768 devices in a mesh: st: 24 (over x, z_hi, core), fifth: 32 (over y, z_lo).
Axes of the slice: x: 4, y: 8, z: 12 (z_hi: 3, z_lo: 4; z = z_hi * 4 + z_lo), core: 2. Of those that a mesh axis runs over, the one named last changes fastest.
Arguments:
- source_field: float32 [2, 4, 3, 32, 24, 4096], P(None, None, None, 'fifth', 'st'), may hold values from -6 to 6
- gauge_rows: float32 [2, 4, 2, 3, 24, 4096], P(None, None, None, None, 'st', 'fifth'), may hold values from -3 to 3
Outputs:
- applied_once: float32 [2, 4, 3, 32, 24, 4096], P(None, None, None, 'fifth', 'st')
- applied_twice: float32 [2, 4, 3, 32, 24, 4096], P(None, None, None, 'fifth', 'st')
The draws below stay inside these ranges and needn't reach their ends.
All inputs are finite; a program needn't handle non-finite values.
Results may differ from the reference program's by a relative error of at most 0.00002.
Values sent between devices are 32-bit elements; how exact they have to be, the bound alone decides.
No kernel may reach another device: no remote copies, remote signals or barrier semaphores. Data moves between devices by JAX's collectives and lax.ppermute only.
A program may use at most 32 MiB of HBM per device.

```python
import jax
import jax.numpy as jnp
import numpy as np
from jax import lax

LS = 16
S3 = 4096
NT = 24
L5 = 32


def shard_levels(stream_key, extent, split, least, top_value):
    def one(position, parts):
        draws = jax.random.uniform(jax.random.fold_in(jax.random.fold_in(stream_key, 6), position), (parts,), jnp.float32, least / len(split), top_value / len(split))
        return jnp.repeat(jnp.exp(draws), extent[position] // parts).reshape((-1,) + (1,) * (len(extent) - position - 1))

    loudness = one(*split[0])
    for cut in split[1:]:
        loudness = loudness * one(*cut)
    return loudness


def scatter_about(key, dims, scale, reach, split=(), kind=jnp.bfloat16):
    level = shard_levels(key, dims, split, -0.22, 0.18) if split else 1.0
    drawn = jax.random.normal(key, dims, jnp.float32) * scale * level
    return jnp.minimum(jnp.maximum(drawn, -reach), reach).astype(kind)


def setup_inputs(seed: int = 0) -> dict:
    splits = jax.random.split(jax.random.key(seed), 3)
    source_field = scatter_about(splits[0], (2, 4, 3, L5, NT, S3), 1.0, 6.0, ((3, 32), (4, 24)), jnp.float32)
    gauge_rows = scatter_about(splits[1], (2, 4, 2, 3, NT, S3), 0.45, 3.0, ((4, 24), (5, 32)), jnp.float32)
    return {"source_field": source_field, "gauge_rows": gauge_rows}


def gamma_tables():
    pauli_real = [np.array([[0.0, 1.0], [1.0, 0.0]]), np.zeros((2, 2)), np.array([[1.0, 0.0], [0.0, -1.0]])]
    pauli_imag = [np.zeros((2, 2)), np.array([[0.0, -1.0], [1.0, 0.0]]), np.zeros((2, 2))]
    real_blocks = []
    imag_blocks = []
    for k in range(3):
        real_matrix = np.zeros((4, 4))
        imag_matrix = np.zeros((4, 4))
        real_matrix[0:2, 2:4] = pauli_imag[k]
        imag_matrix[0:2, 2:4] = -pauli_real[k]
        real_matrix[2:4, 0:2] = -pauli_imag[k]
        imag_matrix[2:4, 0:2] = pauli_real[k]
        real_blocks.append(real_matrix)
        imag_blocks.append(imag_matrix)
    timelike = np.zeros((4, 4))
    timelike[0:2, 2:4] = np.eye(2)
    timelike[2:4, 0:2] = np.eye(2)
    real_blocks.append(timelike)
    imag_blocks.append(np.zeros((4, 4)))
    return np.stack(real_blocks), np.stack(imag_blocks)


GAMMA_REAL, GAMMA_IMAG = gamma_tables()
WALL_HEIGHT = 1.8
QUARK_MASS = 0.5


def complete_links(gauge_rows):
    first_real, first_imag = gauge_rows[0, :, 0], gauge_rows[1, :, 0]
    second_real, second_imag = gauge_rows[0, :, 1], gauge_rows[1, :, 1]
    real_parts = []
    imag_parts = []
    for a in range(3):
        b = (a + 1) % 3
        c = (a + 2) % 3
        real_value = (first_real[:, b] * second_real[:, c] - first_imag[:, b] * second_imag[:, c]) - (first_real[:, c] * second_real[:, b] - first_imag[:, c] * second_imag[:, b])
        imag_value = (first_real[:, b] * second_imag[:, c] + first_imag[:, b] * second_real[:, c]) - (first_real[:, c] * second_imag[:, b] + first_imag[:, c] * second_real[:, b])
        real_parts.append(real_value)
        imag_parts.append(-imag_value)
    last_row = jnp.stack([jnp.stack(real_parts, axis=1), jnp.stack(imag_parts, axis=1)])
    return jnp.concatenate([gauge_rows, last_row[:, :, None]], axis=2)


def adjoint(link):
    return jnp.stack([jnp.swapaxes(link[0], 0, 1), -jnp.swapaxes(link[1], 0, 1)])


def colour_product(link, field):
    real_sum = None
    imag_sum = None
    for b in range(3):
        link_real = link[0][:, b][None, :, None]
        link_imag = link[1][:, b][None, :, None]
        field_real = field[0][:, b:b + 1]
        field_imag = field[1][:, b:b + 1]
        real_term = link_real * field_real - link_imag * field_imag
        imag_term = link_real * field_imag + link_imag * field_real
        real_sum = real_term if real_sum is None else real_sum + real_term
        imag_sum = imag_term if imag_sum is None else imag_sum + imag_term
    return jnp.stack([real_sum, imag_sum])


def spin_project(direction, factor, field):
    real_rows = []
    imag_rows = []
    for i in range(4):
        real_value = field[0, i]
        imag_value = field[1, i]
        for j in range(4):
            coeff_real = float(factor * GAMMA_REAL[direction, i, j])
            coeff_imag = float(factor * GAMMA_IMAG[direction, i, j])
            if coeff_real != 0.0:
                real_value = real_value + coeff_real * field[0, j]
                imag_value = imag_value + coeff_real * field[1, j]
            if coeff_imag != 0.0:
                real_value = real_value - coeff_imag * field[1, j]
                imag_value = imag_value + coeff_imag * field[0, j]
        real_rows.append(real_value)
        imag_rows.append(imag_value)
    return jnp.stack([jnp.stack(real_rows), jnp.stack(imag_rows)])


def neighbour(field, stride, offset):
    coords = (jnp.arange(field.shape[-1]) // stride) % LS
    if offset > 0:
        at_edge = coords == LS - 1
        shifted = jnp.roll(field, -stride, axis=-1)
        wrapped = jnp.roll(field, stride * (LS - 1), axis=-1)
    else:
        at_edge = coords == 0
        shifted = jnp.roll(field, stride, axis=-1)
        wrapped = jnp.roll(field, -stride * (LS - 1), axis=-1)
    return jnp.where(at_edge, wrapped, shifted)


def spatial_hops(field, gauge_field):
    summed = None
    for k in range(3):
        stride = LS ** k
        link = gauge_field[:, k]
        forward = neighbour(field, stride, 1)
        behind = neighbour(field, stride, -1)
        back_link = neighbour(link, stride, -1)
        term = colour_product(link, spin_project(k, -1.0, forward)) + colour_product(adjoint(back_link), spin_project(k, 1.0, behind))
        summed = term if summed is None else summed + term
    return summed


def wilson_hops(field, gauge_field):
    summed = spatial_hops(field, gauge_field)
    time_link = gauge_field[:, 3]
    slots = jnp.arange(NT)
    ahead_factor = jnp.where(slots == NT - 1, -1.0, 1.0)[:, None]
    behind_factor = jnp.where(slots == 0, -1.0, 1.0)[:, None]
    forward = jnp.roll(field, -1, axis=4) * ahead_factor
    behind = jnp.roll(field, 1, axis=4) * behind_factor
    back_link = jnp.roll(time_link, 1, axis=3)
    summed = summed + colour_product(time_link, spin_project(3, -1.0, forward))
    summed = summed + colour_product(adjoint(back_link), spin_project(3, 1.0, behind))
    return summed


def apply_dirac(spinor, gauge_field):
    slices = jnp.moveaxis(spinor, 3, 0)
    hopped = lax.map(lambda piece: wilson_hops(piece[:, :, :, None], gauge_field)[:, :, :, 0], slices)
    hopped = jnp.moveaxis(hopped, 0, 3)
    upper_spins = spinor[:, :2]
    lower_spins = spinor[:, 2:]
    fifth = jnp.arange(L5)
    next_factor = jnp.where(fifth == L5 - 1, -QUARK_MASS, 1.0)[:, None, None]
    prev_factor = jnp.where(fifth == 0, -QUARK_MASS, 1.0)[:, None, None]
    next_lower = jnp.roll(lower_spins, -1, axis=3) * next_factor
    prev_upper = jnp.roll(upper_spins, 1, axis=3) * prev_factor
    chiral = jnp.concatenate([prev_upper, next_lower], axis=1)
    return (5.0 - WALL_HEIGHT) * spinor - 0.5 * hopped - chiral


def reference(source_field, gauge_rows):
    gauge_field = complete_links(gauge_rows)
    applied_once = apply_dirac(source_field, gauge_field)
    applied_twice = apply_dirac(applied_once, gauge_field)
    return (applied_once, applied_twice)
```

```python
import jax
import jax.numpy as jnp
from jax import lax
from jax.experimental import pallas as pl
from jax.experimental.pallas import tpu as pltpu
from jax.sharding import PartitionSpec as P


WALL_HEIGHT = 1.8
QUARK_MASS = 0.5
KS = range(4)
F32 = jnp.float32


def cmul(a, b):
    return a[0] * b[0] - a[1] * b[1], a[0] * b[1] + a[1] * b[0]


def cmul_conj(a, b):
    return a[0] * b[0] + a[1] * b[1], a[0] * b[1] - a[1] * b[0]


def cadd(a, b):
    return a[0] + b[0], a[1] + b[1]


def csub(a, b):
    return a[0] - b[0], a[1] - b[1]


def times_i(a):
    return -a[1], a[0]


def neg(a):
    return -a[0], -a[1]


def row_source(direction, spin):
    if direction == 0:
        return 1 - spin, times_i
    if direction == 1:
        return (1, lambda a: a) if spin == 0 else (0, neg)
    return (0, times_i) if spin == 0 else (1, lambda a: neg(times_i(a)))


def link_index(part, mu, row, col):
    return ((part * 4 + mu) * 2 + row) * 3 + col


TIME_BLOCK = ((18, 24), (42, 48), (0, 4))
SPACE_BLOCK = ((4, 18), (24, 42))
PLACES = {}
for number, spans in enumerate((TIME_BLOCK, SPACE_BLOCK)):
    filled = 0
    for low, high in spans:
        for component in range(low, high):
            PLACES[component] = (number, filled)
            filled += 1


def block_rows(spans):
    return sum(high - low for low, high in spans)


def third_row(rows):
    out = []
    for a in range(3):
        b, c = (a + 1) % 3, (a + 2) % 3
        re, im = csub(cmul(rows[0][b], rows[1][c]), cmul(rows[0][c], rows[1][b]))
        out.append((re, -im))
    return out


def complete(blocks, directions, links):
    for n, mu in enumerate(directions):
        for k in KS:

            def entry(p, r, c):
                number, place = PLACES[link_index(p, mu, r, c)]
                block = blocks[number]
                rows = block.shape[0] // 32
                return block[pl.ds(k * rows + place, 8, stride=4 * rows), :]

            rows = [[(entry(0, r, c), entry(1, r, c)) for c in range(3)] for r in range(2)]
            rows.append(third_row(rows))
            for r in range(3):
                for c in range(3):
                    for p in range(2):
                        links[n, (r * 3 + c) * 2 + p, k] = rows[r][c][p]


def load_link(links, mu, k):
    ref, n = (links[0], mu) if mu < 3 else (links[1], 0)
    return [
        [(ref[n, (r * 3 + c) * 2, k], ref[n, (r * 3 + c) * 2 + 1, k]) for c in range(3)]
        for r in range(3)
    ]


def apply_link(link, half):
    out = []
    for a in range(3):
        total = cmul(link[a][0], half[0])
        for b in (1, 2):
            total = cadd(total, cmul(link[a][b], half[b]))
        out.append(total)
    return out


def apply_adjoint(link, half):
    out = []
    for a in range(3):
        total = cmul_conj(link[0][a], half[0])
        for b in (1, 2):
            total = cadd(total, cmul_conj(link[b][a], half[b]))
        out.append(total)
    return out


def comp(part, spin, colour):
    return (part * 4 + spin) * 3 + colour


def hcomp(part, spin, colour):
    return (part * 2 + spin) * 3 + colour


def get(ref, k, spin):
    at = pl.ds(k, 8, stride=4)
    return [(ref[comp(0, spin, c), at, :], ref[comp(1, spin, c), at, :]) for c in range(3)]


def get_half(ref, k, spin):
    at = pl.ds(8 * k, 8)
    return [(ref[hcomp(0, spin, c), at, :], ref[hcomp(1, spin, c), at, :]) for c in range(3)]


def put_half(ref, k, spin, values):
    at = pl.ds(8 * k, 8)
    for c in range(3):
        ref[hcomp(0, spin, c), at, :] = values[c][0]
        ref[hcomp(1, spin, c), at, :] = values[c][1]


def project(v, k, mu, spin, sign):
    source, factor = row_source(mu, spin)
    upper = get(v, k, spin)
    lower = get(v, k, 2 + source)
    op = cadd if sign > 0 else csub
    return [op(upper[c], factor(lower[c])) for c in range(3)]


def both(fn, *values):
    return [tuple(fn(*(v[c][p] for v in values)) for p in range(2)) for c in range(3)]


def shift_ahead(mu, k, here, other, lane):
    if mu == 0:
        return both(
            lambda h: jnp.where(lane % 16 < 15, pltpu.roll(h, 127, 1), pltpu.roll(h, 15, 1)), here
        )
    if mu == 1:
        return both(lambda h, o: pltpu.roll(jnp.where(lane >= 16, h, o), 112, 1), here, other)
    return other if k < 2 else both(lambda o: pltpu.roll(o, 7, 0), other)


def shift_behind(mu, k, here, other, lane):
    if mu == 0:
        return both(
            lambda h: jnp.where(lane % 16 > 0, pltpu.roll(h, 1, 1), pltpu.roll(h, 113, 1)), here
        )
    if mu == 1:
        return both(lambda h, o: pltpu.roll(jnp.where(lane < 112, h, o), 16, 1), here, other)
    return other if k >= 2 else both(lambda o: pltpu.roll(o, 1, 0), other)


def pick(test, a, b):
    return both(lambda x, y: jnp.where(test, x, y), a, b)


def put_swapped(first, second, k, spin, even, up, down):
    put_half(first, k, spin, pick(even, up, down))
    put_half(second, k, spin, pick(even, down, up))


def even_at(axis):
    return lax.rem(lax.axis_index(axis), 2) == 0


def factors():
    t, s = lax.axis_index("st"), lax.axis_index("fifth")
    nt, ns = lax.axis_size("st"), lax.axis_size("fifth")
    pick = lambda test, value: jnp.where(test, jnp.float32(value), jnp.float32(1.0))
    return (
        pick(t == nt - 1, -1.0),
        pick(t == 0, -1.0),
        pick(s == ns - 1, -QUARK_MASS),
        pick(s == 0, -QUARK_MASS),
    )


def spatial(v, links, moved):
    lane = lax.broadcasted_iota(jnp.int32, (8, 128), 1)
    for k in KS:
        for mu in (1, 2):
            link = load_link(links, mu, k)
            for spin in range(2):
                w = apply_adjoint(link, project(v, k, mu, spin, -1))
                put_half(moved.at[mu - 1], k, spin, w)
    for k in KS:
        hops = [None] * 4
        for mu in range(3):
            link = load_link(links, mu, k)
            partner = (k, k ^ 1, k ^ 2)[mu]
            for spin in range(2):
                here = project(v, k, mu, spin, 1) if mu < 2 else None
                other = project(v, partner, mu, spin, 1) if mu > 0 else None
                fwd = apply_link(link, shift_ahead(mu, k, here, other, lane))
                if mu == 0:
                    w, w_other = apply_adjoint(link, project(v, k, 0, spin, -1)), None
                else:
                    w = get_half(moved.at[mu - 1], k, spin) if mu == 1 else None
                    w_other = get_half(moved.at[mu - 1], partner, spin)
                add_hop(hops, spin, fwd, shift_behind(mu, k, w, w_other, lane), mu)
        yield k, hops


def add_hop(hops, spin, fwd, bwd, mu):
    def add(at, value):
        hops[at] = value if hops[at] is None else both(lambda a, b: a + b, hops[at], value)

    add(spin, both(lambda a, b: a + b, fwd, bwd))
    diff = both(lambda a, b: b - a, fwd, bwd)
    if mu == 3:
        add(2 + spin, diff)
    else:
        target = next(s for s in range(2) if row_source(mu, s)[0] == spin)
        add(2 + target, [row_source(mu, target)[1](d) for d in diff])


def put_field(out, k, values):
    at = pl.ds(k, 8, stride=4)
    for spin in range(4):
        for c in range(3):
            for p in range(2):
                out[comp(p, spin, c), at, :] = values[spin][c][p]


def finish(v, k, hops, links, time1, time2, fifth1, fifth2):
    even_t, even_s = even_at("st"), even_at("fifth")
    time_last, time_first, fifth_last, fifth_first = factors()
    link = load_link(links, 3, k)
    for spin in range(2):
        got1, got2 = get_half(time1, k, spin), get_half(time2, k, spin)
        fwd = apply_link(link, both(lambda a: a * time_last, pick(even_t, got1, got2)))
        bwd = both(lambda a: a * time_first, pick(even_t, got2, got1))
        add_hop(hops, spin, fwd, bwd, 3)
    result = []
    for spin in range(4):
        got1, got2 = get_half(fifth1, k, spin % 2), get_half(fifth2, k, spin % 2)
        if spin < 2:
            chiral, factor = pick(even_s, got2, got1), fifth_first
        else:
            chiral, factor = pick(even_s, got1, got2), fifth_last
        result.append(
            both(
                lambda a, h, c: (5.0 - WALL_HEIGHT) * a - 0.5 * h - c * factor,
                get(v, k, spin), hops[spin], chiral,
            )
        )
    return result


def put_time(time1, time2, k, spin, upper, lower, link):
    diff = both(lambda a, b: a - b, upper, lower)
    moved = apply_adjoint(link, both(lambda a, b: a + b, upper, lower))
    put_swapped(time1, time2, k, spin, even_at("st"), moved, diff)


def fifth_sends(v, fifth1, fifth2):
    for k in KS:
        for spin in range(2):
            put_swapped(fifth1, fifth2, k, spin, even_at("fifth"), get(v, k, spin), get(v, k, 2 + spin))


def time_sends(v, time_block, time1, time2, links):
    complete((time_block, None), (3,), links)
    for k in KS:
        link = load_link((None, links), 3, k)
        for spin in range(2):
            put_time(time1, time2, k, spin, get(v, k, spin), get(v, k, 2 + spin), link)


def first_kernel(
    v, time_block, space_block, time_links, time1, time2, fifth1, fifth2,
    out, kept, space_links, time1_out, time2_out, fifth1_out, fifth2_out, moved,
):
    complete((time_block, space_block), range(3), space_links)
    links = (space_links, time_links)
    for k, hops in spatial(v, links, moved):
        result = finish(v, k, hops, links, time1, time2, fifth1, fifth2)
        put_field(out, k, result)
        put_field(kept, k, result)
        link = load_link(links, 3, k)
        for spin in range(2):
            upper, lower = result[spin], result[2 + spin]
            put_time(time1_out, time2_out, k, spin, upper, lower, link)
            put_swapped(fifth1_out, fifth2_out, k, spin, even_at("fifth"), upper, lower)


def local_kernel(v, space_links, hops_out, moved):
    for k, hops in spatial(v, (space_links, None), moved):
        put_field(hops_out, k, hops)


def second_kernel(v, hops_in, time_links, time1, time2, fifth1, fifth2, out):
    for k in KS:
        hops = [get(hops_in, k, spin) for spin in range(4)]
        put_field(out, k, finish(v, k, hops, (None, time_links), time1, time2, fifth1, fifth2))


def copies_kernel(own, time_out, space_out):
    for spans, out in ((TIME_BLOCK, time_out), (SPACE_BLOCK, space_out)):
        filled = 0
        for low, high in spans:
            out[0, pl.ds(filled, high - low), :] = own[pl.ds(low, high - low), :]
            filled += high - low
        for i in range(1, out.shape[0]):
            out[i] = out[0]


FIELD = jax.ShapeDtypeStruct((24, 32, 128), F32)
HALF = jax.ShapeDtypeStruct((12, 32, 128), F32)
SPACE_LINKS = jax.ShapeDtypeStruct((3, 18, 4, 8, 128), F32)
TIME_LINKS = jax.ShapeDtypeStruct((1, 18, 4, 8, 128), F32)
MOVED = pltpu.VMEM((2, 12, 32, 128), F32)


def run(kernel, outs, scratch, *args):
    size = 4 * sum(a.size for a in args) + 4 * sum(o.size for o in outs)
    vmem = pl.BlockSpec(memory_space=pltpu.VMEM)
    return pl.pallas_call(
        kernel,
        out_shape=outs,
        in_specs=[vmem] * len(args),
        out_specs=[vmem] * len(outs),
        scratch_shapes=scratch,
        cost_estimate=pl.CostEstimate(flops=20_000_000, bytes_accessed=size, transcendentals=0),
        compiler_params=pltpu.CompilerParams(vmem_limit_bytes=24 << 20),
    )(*args)


def trade(block, axis, round):
    count = lax.axis_size(axis)
    step = 1 if round == 1 else -1
    route = [(i, (i + (step if i % 2 == 0 else -step)) % count) for i in range(count)]
    return lax.ppermute(block, axis, route)


def everywhere(copies, axis):
    got = lax.all_to_all(copies, axis, 0, 0, tiled=False)
    return got.reshape(got.shape[0] * got.shape[1], 128)


def on_device(source_field, gauge_rows):
    v = source_field.reshape(24, 32, 128)
    count = lax.axis_size("fifth")
    time_copies, space_copies = run(
        copies_kernel,
        [jax.ShapeDtypeStruct((count, block_rows(b), 128), F32) for b in (TIME_BLOCK, SPACE_BLOCK)],
        [], gauge_rows.reshape(48, 128),
    )
    time_block = everywhere(time_copies, "fifth")
    fifth1, fifth2 = run(fifth_sends, (HALF,) * 2, [], v)
    fifth1 = trade(fifth1, "fifth", 1)
    fifth2 = trade(fifth2, "fifth", 2)
    space_block = everywhere(space_copies, "fifth")
    time1, time2, time_links = run(time_sends, (HALF, HALF, TIME_LINKS), [], v, time_block)
    time1 = trade(time1, "st", 1)
    time2 = trade(time2, "st", 2)
    once, kept, space_links, time1, time2, fifth1, fifth2 = run(
        first_kernel, (FIELD, FIELD, SPACE_LINKS, HALF, HALF, HALF, HALF), [MOVED],
        v, time_block, space_block, time_links, time1, time2, fifth1, fifth2,
    )
    time1 = trade(time1, "st", 1)
    time2 = trade(time2, "st", 2)
    fifth1 = trade(fifth1, "fifth", 1)
    fifth2 = trade(fifth2, "fifth", 2)
    (hops,) = run(local_kernel, (FIELD,), [MOVED], kept, space_links)
    (twice,) = run(second_kernel, (FIELD,), [], kept, hops, time_links, time1, time2, fifth1, fifth2)
    shape = source_field.shape
    return once.reshape(shape), twice.reshape(shape)


def solution(mesh):
    in_specs = (P(None, None, None, "fifth", "st", None), P(None, None, None, None, "st", "fifth"))
    out_specs = (P(None, None, None, "fifth", "st", None), P(None, None, None, "fifth", "st", None))

    return jax.shard_map(on_device, mesh=mesh, in_specs=in_specs, out_specs=out_specs, check_vma=False)
```

```python
import functools

import jax
import jax.numpy as jnp
from jax import lax
from jax.experimental import pallas as pl
from jax.experimental.pallas import tpu as pltpu
from jax.sharding import PartitionSpec as P


WALL_HEIGHT = 1.8
QUARK_MASS = 0.5
KS = range(4)
RUN = 4
F32 = jnp.float32


def cmul(a, b):
    return a[0] * b[0] - a[1] * b[1], a[0] * b[1] + a[1] * b[0]


def cmul_conj(a, b):
    return a[0] * b[0] + a[1] * b[1], a[0] * b[1] - a[1] * b[0]


def cadd(a, b):
    return a[0] + b[0], a[1] + b[1]


def csub(a, b):
    return a[0] - b[0], a[1] - b[1]


def times_i(a):
    return -a[1], a[0]


def neg(a):
    return -a[0], -a[1]


def row_source(direction, spin):
    if direction == 0:
        return 1 - spin, times_i
    if direction == 1:
        return (1, lambda a: a) if spin == 0 else (0, neg)
    return (0, times_i) if spin == 0 else (1, lambda a: neg(times_i(a)))


def link_index(part, mu, row, col):
    return ((part * 4 + mu) * 2 + row) * 3 + col


TIME_BLOCK = ((18, 24), (42, 48))
SPACE_BLOCK = ((0, 18), (24, 42))
PLACES = {}
for number, spans in enumerate((TIME_BLOCK, SPACE_BLOCK)):
    filled = 0
    for low, high in spans:
        for component in range(low, high):
            PLACES[component] = (number, filled)
            filled += 1


def block_rows(spans):
    return sum(high - low for low, high in spans)


def third_row(rows):
    out = []
    for a in range(3):
        b, c = (a + 1) % 3, (a + 2) % 3
        re, im = csub(cmul(rows[0][b], rows[1][c]), cmul(rows[0][c], rows[1][b]))
        out.append((re, -im))
    return out


def complete(blocks, directions, links):
    for n, mu in enumerate(directions):
        for k in KS:

            def entry(p, r, c):
                number, place = PLACES[link_index(p, mu, r, c)]
                block = blocks[number]
                rows = block.shape[0] // 32
                return block[pl.ds(k * rows + place, 8, stride=4 * rows), :]

            rows = [[(entry(0, r, c), entry(1, r, c)) for c in range(3)] for r in range(2)]
            rows.append(third_row(rows))
            for r in range(3):
                for c in range(3):
                    for p in range(2):
                        links[n, (r * 3 + c) * 2 + p, k] = rows[r][c][p]


def load_link(links, mu, k):
    ref, n = (links[0], mu) if mu < 3 else (links[1], 0)
    return [
        [(ref[n, (r * 3 + c) * 2, k], ref[n, (r * 3 + c) * 2 + 1, k]) for c in range(3)]
        for r in range(3)
    ]


def apply_link(link, half):
    out = []
    for a in range(3):
        total = cmul(link[a][0], half[0])
        for b in (1, 2):
            total = cadd(total, cmul(link[a][b], half[b]))
        out.append(total)
    return out


def apply_adjoint(link, half):
    out = []
    for a in range(3):
        total = cmul_conj(link[0][a], half[0])
        for b in (1, 2):
            total = cadd(total, cmul_conj(link[b][a], half[b]))
        out.append(total)
    return out


def comp(part, spin, colour):
    return (part * 4 + spin) * 3 + colour


def hcomp(part, spin, colour):
    return (part * 2 + spin) * 3 + colour


def get(ref, k, spin):
    at = pl.ds(k, 8, stride=4)
    return [(ref[comp(0, spin, c), at, :], ref[comp(1, spin, c), at, :]) for c in range(3)]


def get_half(ref, k, spin):
    at = pl.ds(8 * k, 8)
    return [(ref[hcomp(0, spin, c), at, :], ref[hcomp(1, spin, c), at, :]) for c in range(3)]


def put_half(ref, k, spin, values):
    at = pl.ds(8 * k, 8)
    for c in range(3):
        ref[hcomp(0, spin, c), at, :] = values[c][0]
        ref[hcomp(1, spin, c), at, :] = values[c][1]


def project(v, k, mu, spin, sign):
    source, factor = row_source(mu, spin)
    upper = get(v, k, spin)
    lower = get(v, k, 2 + source)
    op = cadd if sign > 0 else csub
    return [op(upper[c], factor(lower[c])) for c in range(3)]


def both(fn, *values):
    return [tuple(fn(*(v[c][p] for v in values)) for p in range(2)) for c in range(3)]


def shift_ahead(mu, k, here, other, lane):
    if mu == 0:
        return both(
            lambda h: jnp.where(lane % 16 < 15, pltpu.roll(h, 127, 1), pltpu.roll(h, 15, 1)), here
        )
    if mu == 1:
        return both(lambda h, o: pltpu.roll(jnp.where(lane >= 16, h, o), 112, 1), here, other)
    return other if k < 2 else both(lambda o: pltpu.roll(o, 7, 0), other)


def shift_behind(mu, k, here, other, lane):
    if mu == 0:
        return both(
            lambda h: jnp.where(lane % 16 > 0, pltpu.roll(h, 1, 1), pltpu.roll(h, 113, 1)), here
        )
    if mu == 1:
        return both(lambda h, o: pltpu.roll(jnp.where(lane < 112, h, o), 16, 1), here, other)
    return other if k >= 2 else both(lambda o: pltpu.roll(o, 1, 0), other)


def pick(test, a, b):
    return both(lambda x, y: jnp.where(test, x, y), a, b)


def put_swapped(first, second, k, spin, even, up, down):
    put_half(first, k, spin, pick(even, up, down))
    put_half(second, k, spin, pick(even, down, up))


def even_at(axis):
    return lax.rem(lax.axis_index(axis), 2) == 0


def factors():
    t, s = lax.axis_index("st"), lax.axis_index("fifth")
    nt, ns = lax.axis_size("st"), lax.axis_size("fifth")
    pick = lambda test, value: jnp.where(test, jnp.float32(value), jnp.float32(1.0))
    return (
        pick(t == nt - 1, -1.0),
        pick(t == 0, -1.0),
        pick(s == ns - 1, -QUARK_MASS),
        pick(s == 0, -QUARK_MASS),
    )


def spatial(v, links, moved):
    lane = lax.broadcasted_iota(jnp.int32, (8, 128), 1)
    for k in KS:
        for mu in (1, 2):
            link = load_link(links, mu, k)
            for spin in range(2):
                w = apply_adjoint(link, project(v, k, mu, spin, -1))
                put_half(moved.at[mu - 1], k, spin, w)
    for k in KS:
        hops = [None] * 4
        for mu in range(3):
            link = load_link(links, mu, k)
            partner = (k, k ^ 1, k ^ 2)[mu]
            for spin in range(2):
                here = project(v, k, mu, spin, 1) if mu < 2 else None
                other = project(v, partner, mu, spin, 1) if mu > 0 else None
                fwd = apply_link(link, shift_ahead(mu, k, here, other, lane))
                if mu == 0:
                    w, w_other = apply_adjoint(link, project(v, k, 0, spin, -1)), None
                else:
                    w = get_half(moved.at[mu - 1], k, spin) if mu == 1 else None
                    w_other = get_half(moved.at[mu - 1], partner, spin)
                add_hop(hops, spin, fwd, shift_behind(mu, k, w, w_other, lane), mu)
        yield k, hops


def add_hop(hops, spin, fwd, bwd, mu):
    def add(at, value):
        hops[at] = value if hops[at] is None else both(lambda a, b: a + b, hops[at], value)

    add(spin, both(lambda a, b: a + b, fwd, bwd))
    diff = both(lambda a, b: b - a, fwd, bwd)
    if mu == 3:
        add(2 + spin, diff)
    else:
        target = next(s for s in range(2) if row_source(mu, s)[0] == spin)
        add(2 + target, [row_source(mu, target)[1](d) for d in diff])


def put_field(out, k, values):
    at = pl.ds(k, 8, stride=4)
    for spin in range(4):
        for c in range(3):
            for p in range(2):
                out[comp(p, spin, c), at, :] = values[spin][c][p]


def finish(v, k, hops, links, time1, time2, fifth1, fifth2):
    even_t, even_s = even_at("st"), even_at("fifth")
    time_last, time_first, fifth_last, fifth_first = factors()
    link = load_link(links, 3, k)
    for spin in range(2):
        got1, got2 = get_half(time1, k, spin), get_half(time2, k, spin)
        fwd = apply_link(link, both(lambda a: a * time_last, pick(even_t, got1, got2)))
        bwd = both(lambda a: a * time_first, pick(even_t, got2, got1))
        add_hop(hops, spin, fwd, bwd, 3)
    result = []
    for spin in range(4):
        got1, got2 = get_half(fifth1, k, spin % 2), get_half(fifth2, k, spin % 2)
        if spin < 2:
            chiral, factor = pick(even_s, got2, got1), fifth_first
        else:
            chiral, factor = pick(even_s, got1, got2), fifth_last
        result.append(
            both(
                lambda a, h, c: (5.0 - WALL_HEIGHT) * a - 0.5 * h - c * factor,
                get(v, k, spin), hops[spin], chiral,
            )
        )
    return result


def put_time(time1, time2, k, spin, upper, lower, link):
    diff = both(lambda a, b: a - b, upper, lower)
    moved = apply_adjoint(link, both(lambda a, b: a + b, upper, lower))
    put_swapped(time1, time2, k, spin, even_at("st"), moved, diff)


def fifth_sends(v, fifth1, fifth2):
    for k in KS:
        for spin in range(2):
            put_swapped(fifth1, fifth2, k, spin, even_at("fifth"), get(v, k, spin), get(v, k, 2 + spin))


def time_sends(v, time_block, time1, time2, links):
    complete((time_block, None), (3,), links)
    for k in KS:
        link = load_link((None, links), 3, k)
        for spin in range(2):
            put_time(time1, time2, k, spin, get(v, k, spin), get(v, k, 2 + spin), link)


def first_local(v, time_block, space_block, space_links, hops_out, moved):
    complete((time_block, space_block), range(3), space_links)
    for k, hops in spatial(v, (space_links, None), moved):
        put_field(hops_out, k, hops)


def first_kernel(
    v, hops_in, time_links, time1, time2, fifth1, fifth2,
    kept, time1_out, time2_out, fifth1_out, fifth2_out,
):
    links = (None, time_links)
    for k in KS:
        hops = [get(hops_in, k, spin) for spin in range(4)]
        result = finish(v, k, hops, links, time1, time2, fifth1, fifth2)
        put_field(kept, k, result)
        link = load_link(links, 3, k)
        for spin in range(2):
            upper, lower = result[spin], result[2 + spin]
            put_time(time1_out, time2_out, k, spin, upper, lower, link)
            put_swapped(fifth1_out, fifth2_out, k, spin, even_at("fifth"), upper, lower)


def second_local(v, space_links, out, hops_out, moved):
    out[...] = v[...]
    for k, hops in spatial(v, (space_links, None), moved):
        put_field(hops_out, k, hops)


def second_kernel(v, hops_in, time_links, time1, time2, fifth1, fifth2, out):
    for k in KS:
        hops = [get(hops_in, k, spin) for spin in range(4)]
        put_field(out, k, finish(v, k, hops, (None, time_links), time1, time2, fifth1, fifth2))


def ring_copies(spans, run_rows, out):
    filled = 0
    for place in range(RUN):
        for low, high in spans:
            out[0, pl.ds(filled, high - low), :] = run_rows[place, pl.ds(low, high - low), :]
            filled += high - low
    for i in range(1, out.shape[0]):
        out[i] = out[0]


FIELD = jax.ShapeDtypeStruct((24, 32, 128), F32)
HALF = jax.ShapeDtypeStruct((12, 32, 128), F32)
SPACE_LINKS = jax.ShapeDtypeStruct((3, 18, 4, 8, 128), F32)
TIME_LINKS = jax.ShapeDtypeStruct((1, 18, 4, 8, 128), F32)
MOVED = pltpu.VMEM((2, 12, 32, 128), F32)


def run(kernel, outs, scratch, *args):
    size = 4 * sum(a.size for a in args) + 4 * sum(o.size for o in outs)
    vmem = pl.BlockSpec(memory_space=pltpu.VMEM)
    return pl.pallas_call(
        kernel,
        out_shape=outs,
        in_specs=[vmem] * len(args),
        out_specs=[vmem] * len(outs),
        scratch_shapes=scratch,
        cost_estimate=pl.CostEstimate(flops=20_000_000, bytes_accessed=size, transcendentals=0),
        compiler_params=pltpu.CompilerParams(vmem_limit_bytes=24 << 20),
    )(*args)


def trade(block, axis, round):
    count = lax.axis_size(axis)
    step = 1 if round == 1 else -1
    route = [(i, (i + (step if i % 2 == 0 else -step)) % count) for i in range(count)]
    return lax.ppermute(block, axis, route)


def traded(copies, groups):
    return lax.all_to_all(copies, "fifth", 0, 0, axis_index_groups=groups, tiled=False)


def ring_traded(copies, groups):
    got = traded(copies, groups)
    return got.reshape(got.shape[0] * got.shape[1], 128)


def on_device(source_field, gauge_rows):
    v = source_field.reshape(24, 32, 128)
    count = lax.axis_size("fifth")
    runs = [list(range(i, i + RUN)) for i in range(0, count, RUN)]
    rings = [list(range(i, count, RUN)) for i in range(RUN)]
    own = jnp.broadcast_to(gauge_rows.reshape(1, 48, 128), (RUN, 48, 128))
    run_rows = traded(own, runs)
    time_copies, space_copies = (
        run(
            functools.partial(ring_copies, spans),
            (jax.ShapeDtypeStruct((count // RUN, RUN * block_rows(spans), 128), F32),), [], run_rows,
        )[0]
        for spans in (TIME_BLOCK, SPACE_BLOCK)
    )
    time_block = ring_traded(time_copies, rings)
    fifth1, fifth2 = run(fifth_sends, (HALF,) * 2, [], v)
    fifth1 = trade(fifth1, "fifth", 1)
    fifth2 = trade(fifth2, "fifth", 2)
    space_block = ring_traded(space_copies, rings)
    time1, time2, time_links = run(time_sends, (HALF, HALF, TIME_LINKS), [], v, time_block)
    time1 = trade(time1, "st", 1)
    time2 = trade(time2, "st", 2)
    space_links, hops = run(first_local, (SPACE_LINKS, FIELD), [MOVED], v, time_block, space_block)
    kept, time1, time2, fifth1, fifth2 = run(
        first_kernel, (FIELD, HALF, HALF, HALF, HALF), [], v, hops, time_links, time1, time2, fifth1, fifth2
    )
    time1 = trade(time1, "st", 1)
    time2 = trade(time2, "st", 2)
    fifth1 = trade(fifth1, "fifth", 1)
    fifth2 = trade(fifth2, "fifth", 2)
    once, hops = run(second_local, (FIELD, FIELD), [MOVED], kept, space_links)
    (twice,) = run(second_kernel, (FIELD,), [], kept, hops, time_links, time1, time2, fifth1, fifth2)
    shape = source_field.shape
    return once.reshape(shape), twice.reshape(shape)


def solution(mesh):
    in_specs = (P(None, None, None, "fifth", "st", None), P(None, None, None, None, "st", "fifth"))
    out_specs = (P(None, None, None, "fifth", "st", None), P(None, None, None, "fifth", "st", None))

    return jax.shard_map(on_device, mesh=mesh, in_specs=in_specs, out_specs=out_specs, check_vma=False)
```

```python
import functools

import jax
import jax.numpy as jnp
from jax import lax
from jax.experimental import pallas as pl
from jax.experimental.pallas import tpu as pltpu
from jax.sharding import PartitionSpec as P


WALL_HEIGHT = 1.8
QUARK_MASS = 0.5
KS = range(4)
RUN = 4
F32 = jnp.float32


def cmul(a, b):
    return a[0] * b[0] - a[1] * b[1], a[0] * b[1] + a[1] * b[0]


def cmul_conj(a, b):
    return a[0] * b[0] + a[1] * b[1], a[0] * b[1] - a[1] * b[0]


def cadd(a, b):
    return a[0] + b[0], a[1] + b[1]


def csub(a, b):
    return a[0] - b[0], a[1] - b[1]


def times_i(a):
    return -a[1], a[0]


def neg(a):
    return -a[0], -a[1]


def row_source(direction, spin):
    if direction == 0:
        return 1 - spin, times_i
    if direction == 1:
        return (1, lambda a: a) if spin == 0 else (0, neg)
    return (0, times_i) if spin == 0 else (1, lambda a: neg(times_i(a)))


def link_index(part, mu, row, col):
    return ((part * 4 + mu) * 2 + row) * 3 + col


TIME_BLOCK = ((18, 24), (42, 48))
SPACE_BLOCK = ((0, 18), (24, 42))
PLACES = {}
for number, spans in enumerate((TIME_BLOCK, SPACE_BLOCK)):
    filled = 0
    for low, high in spans:
        for component in range(low, high):
            PLACES[component] = (number, filled)
            filled += 1


def block_rows(spans):
    return sum(high - low for low, high in spans)


def third_row(rows):
    out = []
    for a in range(3):
        b, c = (a + 1) % 3, (a + 2) % 3
        re, im = csub(cmul(rows[0][b], rows[1][c]), cmul(rows[0][c], rows[1][b]))
        out.append((re, -im))
    return out


def complete(blocks, directions, links):
    for n, mu in enumerate(directions):
        for k in KS:

            def entry(p, r, c):
                number, place = PLACES[link_index(p, mu, r, c)]
                block = blocks[number]
                rows = block.shape[0] // 32
                return block[pl.ds(k * rows + place, 8, stride=4 * rows), :]

            rows = [[(entry(0, r, c), entry(1, r, c)) for c in range(3)] for r in range(2)]
            rows.append(third_row(rows))
            for r in range(3):
                for c in range(3):
                    for p in range(2):
                        links[n, (r * 3 + c) * 2 + p, k] = rows[r][c][p]


def load_link(links, mu, k):
    ref, n = (links[0], mu) if mu < 3 else (links[1], 0)
    return [
        [(ref[n, (r * 3 + c) * 2, k], ref[n, (r * 3 + c) * 2 + 1, k]) for c in range(3)]
        for r in range(3)
    ]


def apply_link(link, half):
    out = []
    for a in range(3):
        total = cmul(link[a][0], half[0])
        for b in (1, 2):
            total = cadd(total, cmul(link[a][b], half[b]))
        out.append(total)
    return out


def apply_adjoint(link, half):
    out = []
    for a in range(3):
        total = cmul_conj(link[0][a], half[0])
        for b in (1, 2):
            total = cadd(total, cmul_conj(link[b][a], half[b]))
        out.append(total)
    return out


def comp(part, spin, colour):
    return (part * 4 + spin) * 3 + colour


def hcomp(part, spin, colour):
    return (part * 2 + spin) * 3 + colour


def get(ref, k, spin):
    at = pl.ds(k, 8, stride=4)
    return [(ref[comp(0, spin, c), at, :], ref[comp(1, spin, c), at, :]) for c in range(3)]


def get_half(ref, k, spin):
    at = pl.ds(8 * k, 8)
    return [(ref[hcomp(0, spin, c), at, :], ref[hcomp(1, spin, c), at, :]) for c in range(3)]


def put_half(ref, k, spin, values):
    at = pl.ds(8 * k, 8)
    for c in range(3):
        ref[hcomp(0, spin, c), at, :] = values[c][0]
        ref[hcomp(1, spin, c), at, :] = values[c][1]


def project(v, k, mu, spin, sign):
    source, factor = row_source(mu, spin)
    upper = get(v, k, spin)
    lower = get(v, k, 2 + source)
    op = cadd if sign > 0 else csub
    return [op(upper[c], factor(lower[c])) for c in range(3)]


def both(fn, *values):
    return [tuple(fn(*(v[c][p] for v in values)) for p in range(2)) for c in range(3)]


def shift_ahead(mu, k, here, other, lane):
    if mu == 0:
        return both(
            lambda h: jnp.where(lane % 16 < 15, pltpu.roll(h, 127, 1), pltpu.roll(h, 15, 1)), here
        )
    if mu == 1:
        return both(lambda h, o: pltpu.roll(jnp.where(lane >= 16, h, o), 112, 1), here, other)
    return other if k < 2 else both(lambda o: pltpu.roll(o, 7, 0), other)


def shift_behind(mu, k, here, other, lane):
    if mu == 0:
        return both(
            lambda h: jnp.where(lane % 16 > 0, pltpu.roll(h, 1, 1), pltpu.roll(h, 113, 1)), here
        )
    if mu == 1:
        return both(lambda h, o: pltpu.roll(jnp.where(lane < 112, h, o), 16, 1), here, other)
    return other if k >= 2 else both(lambda o: pltpu.roll(o, 1, 0), other)


def pick(test, a, b):
    return both(lambda x, y: jnp.where(test, x, y), a, b)


def put_swapped(first, second, k, spin, even, up, down):
    put_half(first, k, spin, pick(even, up, down))
    put_half(second, k, spin, pick(even, down, up))


def even_at(axis):
    return lax.rem(lax.axis_index(axis), 2) == 0


def factors():
    t, s = lax.axis_index("st"), lax.axis_index("fifth")
    nt, ns = lax.axis_size("st"), lax.axis_size("fifth")
    pick = lambda test, value: jnp.where(test, jnp.float32(value), jnp.float32(1.0))
    return (
        pick(t == nt - 1, -1.0),
        pick(t == 0, -1.0),
        pick(s == ns - 1, -QUARK_MASS),
        pick(s == 0, -QUARK_MASS),
    )


def spatial(v, links, moved):
    lane = lax.broadcasted_iota(jnp.int32, (8, 128), 1)
    for k in KS:
        for mu in (1, 2):
            link = load_link(links, mu, k)
            for spin in range(2):
                w = apply_adjoint(link, project(v, k, mu, spin, -1))
                put_half(moved.at[mu - 1], k, spin, w)
    for k in KS:
        hops = [None] * 4
        for mu in range(3):
            link = load_link(links, mu, k)
            partner = (k, k ^ 1, k ^ 2)[mu]
            for spin in range(2):
                here = project(v, k, mu, spin, 1) if mu < 2 else None
                other = project(v, partner, mu, spin, 1) if mu > 0 else None
                fwd = apply_link(link, shift_ahead(mu, k, here, other, lane))
                if mu == 0:
                    w, w_other = apply_adjoint(link, project(v, k, 0, spin, -1)), None
                else:
                    w = get_half(moved.at[mu - 1], k, spin) if mu == 1 else None
                    w_other = get_half(moved.at[mu - 1], partner, spin)
                add_hop(hops, spin, fwd, shift_behind(mu, k, w, w_other, lane), mu)
        yield k, hops


def add_hop(hops, spin, fwd, bwd, mu):
    def add(at, value):
        hops[at] = value if hops[at] is None else both(lambda a, b: a + b, hops[at], value)

    add(spin, both(lambda a, b: a + b, fwd, bwd))
    diff = both(lambda a, b: b - a, fwd, bwd)
    if mu == 3:
        add(2 + spin, diff)
    else:
        target = next(s for s in range(2) if row_source(mu, s)[0] == spin)
        add(2 + target, [row_source(mu, target)[1](d) for d in diff])


def put_field(out, k, values):
    at = pl.ds(k, 8, stride=4)
    for spin in range(4):
        for c in range(3):
            for p in range(2):
                out[comp(p, spin, c), at, :] = values[spin][c][p]


def finish(v, k, hops, links, time1, time2, fifth1, fifth2):
    even_t, even_s = even_at("st"), even_at("fifth")
    time_last, time_first, fifth_last, fifth_first = factors()
    link = load_link(links, 3, k)
    for spin in range(2):
        got1, got2 = get_half(time1, k, spin), get_half(time2, k, spin)
        fwd = apply_link(link, both(lambda a: a * time_last, pick(even_t, got1, got2)))
        bwd = both(lambda a: a * time_first, pick(even_t, got2, got1))
        add_hop(hops, spin, fwd, bwd, 3)
    result = []
    for spin in range(4):
        got1, got2 = get_half(fifth1, k, spin % 2), get_half(fifth2, k, spin % 2)
        if spin < 2:
            chiral, factor = pick(even_s, got2, got1), fifth_first
        else:
            chiral, factor = pick(even_s, got1, got2), fifth_last
        result.append(
            both(
                lambda a, h, c: (5.0 - WALL_HEIGHT) * a - 0.5 * h - c * factor,
                get(v, k, spin), hops[spin], chiral,
            )
        )
    return result


def put_time(time1, time2, k, spin, upper, lower, link):
    diff = both(lambda a, b: a - b, upper, lower)
    moved = apply_adjoint(link, both(lambda a, b: a + b, upper, lower))
    put_swapped(time1, time2, k, spin, even_at("st"), moved, diff)


def fifth_sends(v, fifth1, fifth2):
    for k in KS:
        for spin in range(2):
            put_swapped(fifth1, fifth2, k, spin, even_at("fifth"), get(v, k, spin), get(v, k, 2 + spin))


def time_sends(v, time_block, time1, time2, links):
    complete((time_block, None), (3,), links)
    for k in KS:
        link = load_link((None, links), 3, k)
        for spin in range(2):
            put_time(time1, time2, k, spin, get(v, k, spin), get(v, k, 2 + spin), link)


def first_local(v, time_block, space_block, space_links, hops_out, moved):
    complete((time_block, space_block), range(3), space_links)
    for k, hops in spatial(v, (space_links, None), moved):
        put_field(hops_out, k, hops)


def first_kernel(
    v, hops_in, time_links, time1, time2, fifth1, fifth2,
    kept, time1_out, time2_out, fifth1_out, fifth2_out,
):
    links = (None, time_links)
    for k in KS:
        hops = [get(hops_in, k, spin) for spin in range(4)]
        result = finish(v, k, hops, links, time1, time2, fifth1, fifth2)
        put_field(kept, k, result)
        link = load_link(links, 3, k)
        for spin in range(2):
            upper, lower = result[spin], result[2 + spin]
            put_time(time1_out, time2_out, k, spin, upper, lower, link)
            put_swapped(fifth1_out, fifth2_out, k, spin, even_at("fifth"), upper, lower)


def second_local(v, space_links, out, hops_out, moved):
    out[...] = v[...]
    for k, hops in spatial(v, (space_links, None), moved):
        put_field(hops_out, k, hops)


def second_kernel(v, hops_in, time_links, time1, time2, fifth1, fifth2, out):
    for k in KS:
        hops = [get(hops_in, k, spin) for spin in range(4)]
        put_field(out, k, finish(v, k, hops, (None, time_links), time1, time2, fifth1, fifth2))


def run_copies(own, out, held, sem_in, sem_out):
    load = pltpu.make_async_copy(own, held, sem_in)
    load.start()
    load.wait()
    stores = [pltpu.make_async_copy(held, out.at[i], sem_out.at[i]) for i in range(RUN)]
    for store in stores:
        store.start()
    for store in stores:
        store.wait()


def ring_copies(spans, run_rows, out):
    filled = 0
    for place in range(RUN):
        for low, high in spans:
            out[0, pl.ds(filled, high - low), :] = run_rows[place, pl.ds(low, high - low), :]
            filled += high - low
    for i in range(1, out.shape[0]):
        out[i] = out[0]


FIELD = jax.ShapeDtypeStruct((24, 32, 128), F32)
HALF = jax.ShapeDtypeStruct((12, 32, 128), F32)
SPACE_LINKS = jax.ShapeDtypeStruct((3, 18, 4, 8, 128), F32)
TIME_LINKS = jax.ShapeDtypeStruct((1, 18, 4, 8, 128), F32)
MOVED = pltpu.VMEM((2, 12, 32, 128), F32)


def run(kernel, outs, scratch, *args):
    size = 4 * sum(a.size for a in args) + 4 * sum(o.size for o in outs)
    vmem = pl.BlockSpec(memory_space=pltpu.VMEM)
    return pl.pallas_call(
        kernel,
        out_shape=outs,
        in_specs=[vmem] * len(args),
        out_specs=[vmem] * len(outs),
        scratch_shapes=scratch,
        cost_estimate=pl.CostEstimate(flops=20_000_000, bytes_accessed=size, transcendentals=0),
        compiler_params=pltpu.CompilerParams(vmem_limit_bytes=24 << 20),
    )(*args)


def trade(block, axis, round):
    count = lax.axis_size(axis)
    step = 1 if round == 1 else -1
    route = [(i, (i + (step if i % 2 == 0 else -step)) % count) for i in range(count)]
    return lax.ppermute(block, axis, route)


def traded(copies, groups):
    return lax.all_to_all(copies, "fifth", 0, 0, axis_index_groups=groups, tiled=False)


def ring_traded(copies, groups):
    got = traded(copies, groups)
    return got.reshape(got.shape[0] * got.shape[1], 128)


def on_device(source_field, gauge_rows):
    v = source_field.reshape(24, 32, 128)
    count = lax.axis_size("fifth")
    runs = [list(range(i, i + RUN)) for i in range(0, count, RUN)]
    rings = [list(range(i, count, RUN)) for i in range(RUN)]
    own = pl.pallas_call(
        run_copies,
        out_shape=jax.ShapeDtypeStruct((RUN, 48, 128), F32),
        in_specs=[pl.BlockSpec(memory_space=pl.ANY)],
        out_specs=pl.BlockSpec(memory_space=pl.ANY),
        scratch_shapes=[
            pltpu.VMEM((48, 128), F32), pltpu.SemaphoreType.DMA, pltpu.SemaphoreType.DMA((RUN,))
        ],
    )(gauge_rows.reshape(48, 128))
    run_rows = traded(own, runs)
    time_copies, space_copies = (
        run(
            functools.partial(ring_copies, spans),
            (jax.ShapeDtypeStruct((count // RUN, RUN * block_rows(spans), 128), F32),), [], run_rows,
        )[0]
        for spans in (TIME_BLOCK, SPACE_BLOCK)
    )
    time_block = ring_traded(time_copies, rings)
    fifth1, fifth2 = run(fifth_sends, (HALF,) * 2, [], v)
    fifth1 = trade(fifth1, "fifth", 1)
    fifth2 = trade(fifth2, "fifth", 2)
    space_block = ring_traded(space_copies, rings)
    time1, time2, time_links = run(time_sends, (HALF, HALF, TIME_LINKS), [], v, time_block)
    time1 = trade(time1, "st", 1)
    time2 = trade(time2, "st", 2)
    space_links, hops = run(first_local, (SPACE_LINKS, FIELD), [MOVED], v, time_block, space_block)
    kept, time1, time2, fifth1, fifth2 = run(
        first_kernel, (FIELD, HALF, HALF, HALF, HALF), [], v, hops, time_links, time1, time2, fifth1, fifth2
    )
    time1 = trade(time1, "st", 1)
    time2 = trade(time2, "st", 2)
    fifth1 = trade(fifth1, "fifth", 1)
    fifth2 = trade(fifth2, "fifth", 2)
    once, hops = run(second_local, (FIELD, FIELD), [MOVED], kept, space_links)
    (twice,) = run(second_kernel, (FIELD,), [], kept, hops, time_links, time1, time2, fifth1, fifth2)
    shape = source_field.shape
    return once.reshape(shape), twice.reshape(shape)


def solution(mesh):
    in_specs = (P(None, None, None, "fifth", "st", None), P(None, None, None, None, "st", "fifth"))
    out_specs = (P(None, None, None, "fifth", "st", None), P(None, None, None, "fifth", "st", None))

    return jax.shard_map(on_device, mesh=mesh, in_specs=in_specs, out_specs=out_specs, check_vma=False)
```
